128 devices in a mesh: space: 16 (over z, y), pencil: 8 (over x, core).
Axes of the slice: x: 4, y: 4, z: 4, core: 2. Of those that a mesh axis runs over, the one named last changes fastest.
Arguments:
- species: float32 [2048, 53, 1024], P('space', None, 'pencil'), may hold values from 0 to 1
- diffusivity: float32 [53], replicated, may hold values from 0.03 to 0.24
- propagator: float32 [2048, 22472], P('space', 'pencil'), may hold values from -0.03 to 0.92, as said below
- reaction_rate: float32 [2048, 1024], P('space', 'pencil'), may hold values from 0.02 to 0.2
- substeps: int32 [2048, 8], P('space', 'pencil'), may hold values from 1 to 30, as said below
Outputs:
- reacted: float32 [2048, 53, 1024], P('space', None, 'pencil')
The draws below stay inside these ranges and needn't reach their ends.
Inputs may be any that keep to these rules, and one draw needn't show every extreme that they name: `substeps`: every value lies between 1 and 30, and the largest value, 30, is reached in every draw. `propagator`: each block's matrix has diagonal entries between 0.84 and 0.92 and off-diagonal entries of at most 0.03 in magnitude.
All inputs are finite; a program needn't handle non-finite values.
Results may differ from the reference program's by a relative error of at most 0.0003.
Values sent between devices are 32-bit elements; how exact they have to be, the bound alone decides.
No kernel may reach another device: no remote copies, remote signals or barrier semaphores. Data moves between devices by JAX's collectives and lax.ppermute only.
A program may use at most 128 MiB of HBM per device.

```python
import math
import jax
import jax.numpy as jnp
from jax import lax

NSPEC = 53
BLOCK = 128
SUBMAX = 30
ROWS_DEV = 128
NA = 2048
NB = 1024
N_PENCIL = 8


def draw_propagator(key, part):
    first, second = jax.random.split(jax.random.fold_in(key, 11))
    diagonal = jax.random.uniform(first, (NA, N_PENCIL, NSPEC), jnp.float32, 0.84, 0.92)
    offdiag = 0.01 * jnp.clip(jax.random.normal(second, (NA, N_PENCIL, NSPEC, NSPEC), jnp.float32), -3.0, 3.0)
    identity = jnp.eye(NSPEC, dtype=jnp.float32)
    matrix = offdiag * (1.0 - identity) + diagonal[..., None] * identity
    return matrix.reshape(NA, N_PENCIL * NSPEC * NSPEC).astype(jnp.float32)


def draw_substeps(key, part):
    first, second = jax.random.split(jax.random.fold_in(key, 23))
    center = jax.random.randint(first, (), 0, NA, dtype=jnp.int32)
    positions = jnp.arange(NA, dtype=jnp.int32)
    distance = jnp.abs(positions - center)
    distance = jnp.minimum(distance, NA - distance)
    spread_width = max(1, ROWS_DEV // 7)
    base_count = SUBMAX - distance // spread_width
    jitter = jax.random.randint(second, (NA, N_PENCIL), 0, 3, dtype=jnp.int32)
    jitter = jitter * (distance > 0).astype(jnp.int32)[:, None]
    return jnp.clip(base_count[:, None] - jitter, 1, SUBMAX).astype(jnp.int32)


def block_levels(rng, shape, shards, least, high):
    def one(dim, parts):
        heights = jax.random.uniform(jax.random.fold_in(jax.random.fold_in(rng, 6), dim), (parts,), jnp.float32, least / len(shards), high / len(shards))
        return jnp.repeat(jnp.exp(heights), shape[dim] // parts).reshape((-1,) + (1,) * (len(shape) - dim - 1))

    gain = one(*shards[0])
    for cut in shards[1:]:
        gain = gain * one(*cut)
    return gain


def setup_inputs(seed: int = 0) -> dict:
    key_list = jax.random.split(jax.random.key(seed), 6)
    return {
        "species": jnp.clip(1.0 * jax.random.uniform(key_list[0], (NA, NSPEC, NB), jnp.float32) ** block_levels(key_list[0], (NA, NSPEC, NB), ((0, 16), (2, 8)), -0.2, 0.2), 0.0, 1.0),
        "diffusivity": jnp.clip(jnp.exp(jax.random.uniform(key_list[1], (NSPEC,), jnp.float32, math.log(0.03), math.log(0.24))), 0.03, 0.24),
        "propagator": draw_propagator(jax.random.fold_in(key_list[5], 71), 0),
        "reaction_rate": jnp.clip(jnp.exp(math.log(0.2) - 2.3025851 * jax.random.uniform(key_list[3], (NA, NB), jnp.float32) ** block_levels(key_list[3], (NA, NB), ((0, 16), (1, 8)), -0.2, 0.2)), 0.02, 0.2),
        "substeps": draw_substeps(jax.random.fold_in(key_list[5], 71), 0),
    }


def reference(species, diffusivity, propagator, reaction_rate, substeps):
    neighbours = jnp.roll(species, 1, 0) + jnp.roll(species, -1, 0) + jnp.roll(species, 1, 2) + jnp.roll(species, -1, 2)
    diffused = species + diffusivity[None, :, None] * (neighbours - 4.0 * species)
    block_count = NA * N_PENCIL
    blocks = diffused.reshape(NA, NSPEC, N_PENCIL, BLOCK).transpose(0, 2, 1, 3).reshape(block_count, NSPEC, BLOCK)
    matrices = propagator.reshape(block_count, NSPEC, NSPEC)
    rates = reaction_rate.reshape(block_count, BLOCK)
    counts = substeps.reshape(block_count)
    order = jnp.argsort(-counts, stable=True)
    group_size = 64
    group_count = block_count // group_size
    sorted_blocks = jnp.take(blocks, order, axis=0).reshape(group_count, group_size, NSPEC, BLOCK)
    sorted_mats = jnp.take(matrices, order, axis=0).reshape(group_count, group_size, NSPEC, NSPEC)
    sorted_rates = jnp.take(rates, order, axis=0).reshape(group_count, group_size, BLOCK)
    sorted_counts = jnp.take(counts, order, axis=0).reshape(group_count, group_size)

    def run_group(inputs):
        state, mats, rate_rows, count_rows = inputs

        def substep(step_index, current):
            pushed = current + rate_rows[:, None, :] * jnp.tanh(current)
            fresh = jnp.einsum("gij,gjc->gic", mats, pushed, precision=lax.Precision.HIGHEST)
            return jnp.where((step_index < count_rows)[:, None, None], fresh, current)

        return lax.fori_loop(0, jnp.max(count_rows), substep, state)

    finished = lax.map(run_group, (sorted_blocks, sorted_mats, sorted_rates, sorted_counts))
    inverse = jnp.argsort(order)
    restored = jnp.take(finished.reshape(block_count, NSPEC, BLOCK), inverse, axis=0)
    return restored.reshape(NA, N_PENCIL, NSPEC, BLOCK).transpose(0, 2, 1, 3).reshape(NA, NSPEC, NB)
```

```python
import functools

import jax
import jax.numpy as jnp
from jax import lax
from jax.experimental import pallas as pl
from jax.experimental.pallas import tpu as pltpu
from jax.sharding import PartitionSpec as P

GROUP = 16
UNROLL = 2


def react_kernel(nspec, counts, species, top, bottom, left, right, diff, prop, rate, out, pbuf, lhs, state):
    rows_total = species.shape[0]
    lanes = species.shape[2]
    pad = pbuf.shape[0] // GROUP
    base = pl.program_id(0) * GROUP

    lane = lax.broadcasted_iota(jnp.int32, (nspec, lanes), 1)
    coef = jnp.broadcast_to(diff[...], (nspec, lanes))

    pbuf[...] = jnp.zeros_like(pbuf)
    zeros_tail = jnp.zeros((GROUP, lanes - nspec), jnp.float32)
    for i in range(nspec):
        piece = prop[:, i * nspec : (i + 1) * nspec]
        pbuf[pl.ds(i, GROUP, stride=pad), :] = jnp.concatenate([piece, zeros_tail], axis=1)
    for g in range(GROUP):
        mat = pbuf[g * pad : (g + 1) * pad, :]
        high = mat.astype(jnp.bfloat16)
        high32 = high.astype(jnp.float32)
        low = mat - high32
        both = high32 + pltpu.roll(high32, 64, 1)
        lhs[g, :, 0:lanes] = both.astype(jnp.bfloat16)
        lhs[g, :, lanes : 2 * lanes] = low.astype(jnp.bfloat16)

    state[...] = jnp.zeros_like(state)
    for g in range(GROUP):
        row = base + g
        here = species[row]
        if g == 0:
            above = jnp.where(row == 0, top[...], species[jnp.maximum(row - 1, 0)])
        else:
            above = species[row - 1]
        if g == GROUP - 1:
            below = jnp.where(row == rows_total - 1, bottom[...], species[jnp.minimum(row + 1, rows_total - 1)])
        else:
            below = species[row + 1]
        edge_l = pltpu.roll(left[...], lanes - 1 - row, 1)
        edge_r = pltpu.roll(right[...], lanes - row, 1)
        from_l = pltpu.roll(jnp.where(lane == lanes - 1, edge_l, here), 1, 1)
        from_r = pltpu.roll(jnp.where(lane == 0, edge_r, here), lanes - 1, 1)
        state[g, 0:nspec, :] = here + coef * ((above + below) + (from_l + from_r) - 4.0 * here)

    least = counts[base]
    most = counts[base]
    for g in range(1, GROUP):
        least = jnp.minimum(least, counts[base + g])
        most = jnp.maximum(most, counts[base + g])

    pad_rows = jnp.zeros((64 - 56, lanes), jnp.float32)

    def advance(g):
        now = state[g]
        pushed = now + rate[g : g + 1, :] * jnp.tanh(now)
        full = jnp.concatenate([pushed, pad_rows], axis=0)
        high = full.astype(jnp.bfloat16)
        low = (full - high.astype(jnp.float32)).astype(jnp.bfloat16)
        rhs = jnp.concatenate([high, low, high, jnp.zeros_like(high)], axis=0)
        fresh = jnp.dot(lhs[g], rhs, preferred_element_type=jnp.float32)
        return now, fresh[0:56]

    def all_blocks(step, carry):
        for _ in range(UNROLL):
            for g in range(GROUP):
                state[g] = advance(g)[1]
        return carry

    def some_blocks(step, carry):
        for g in range(GROUP):
            now, fresh = advance(g)
            state[g] = jnp.where(step < counts[base + g], fresh, now)
        return carry

    whole = least // UNROLL
    lax.fori_loop(0, whole, all_blocks, 0)
    lax.fori_loop(whole * UNROLL, most, some_blocks, 0)
    out[...] = state[:, 0:nspec, :]


def body(species, diffusivity, propagator, reaction_rate, substeps):
    rows, nspec, lanes = species.shape

    def shift(cells, axis, up):
        count = lax.axis_size(axis)
        pairs = [(i, (i + 1) % count) if up else ((i + 1) % count, i) for i in range(count)]
        return lax.ppermute(cells, axis, pairs)

    top = shift(species[rows - 1], "space", True)
    bottom = shift(species[0], "space", False)
    left = shift(species[:, :, lanes - 1].T, "pencil", True)
    right = shift(species[:, :, 0].T, "pencil", False)

    pad = 64
    whole3 = pl.BlockSpec((rows, nspec, lanes), lambda i, c: (0, 0, 0), pipeline_mode=pl.Buffered(1))
    whole2 = pl.BlockSpec((nspec, lanes), lambda i, c: (0, 0), pipeline_mode=pl.Buffered(1))
    edge = pl.BlockSpec((nspec, rows), lambda i, c: (0, 0), pipeline_mode=pl.Buffered(1))
    return pl.pallas_call(
        functools.partial(react_kernel, nspec),
        out_shape=jax.ShapeDtypeStruct(species.shape, jnp.float32),
        grid_spec=pltpu.PrefetchScalarGridSpec(
            num_scalar_prefetch=1,
            grid=(rows // GROUP,),
            in_specs=[
                whole3,
                whole2,
                whole2,
                edge,
                edge,
                pl.BlockSpec((nspec, 1), lambda i, c: (0, 0), pipeline_mode=pl.Buffered(1)),
                pl.BlockSpec((GROUP, nspec * nspec), lambda i, c: (i, 0)),
                pl.BlockSpec((GROUP, lanes), lambda i, c: (i, 0)),
            ],
            out_specs=pl.BlockSpec((GROUP, nspec, lanes), lambda i, c: (i, 0, 0)),
            scratch_shapes=[
                pltpu.VMEM((GROUP * pad, lanes), jnp.float32),
                pltpu.VMEM((GROUP, pad, 2 * lanes), jnp.bfloat16),
                pltpu.VMEM((GROUP, 56, lanes), jnp.float32),
            ],
        ),
        compiler_params=pltpu.CompilerParams(vmem_limit_bytes=40 << 20),
        cost_estimate=pl.CostEstimate(flops=rows * 20 * 2 * 64 * 256 * 128, bytes_accessed=9 << 20, transcendentals=0),
    )(
        substeps.reshape(rows),
        species,
        top,
        bottom,
        left,
        right,
        diffusivity.reshape(nspec, 1),
        propagator,
        reaction_rate,
    )


def solution(mesh):
    return jax.shard_map(
        body,
        mesh=mesh,
        in_specs=(
            P("space", None, "pencil"),
            P(),
            P("space", "pencil"),
            P("space", "pencil"),
            P("space", "pencil"),
        ),
        out_specs=P("space", None, "pencil"),
        check_vma=False,
    )
```

```python
import functools

import jax
import jax.numpy as jnp
from jax import lax
from jax.experimental import pallas as pl
from jax.experimental.pallas import tpu as pltpu
from jax.sharding import PartitionSpec as P

EDGE_ROWS = 16
PREP_ROWS = 16
GROUP = 32
UNROLL = 4
LANES = 128


def edges_kernel(nspec, cells, first_col, last_col, first_row, last_row):
    step = pl.program_id(0)
    lane = lax.broadcasted_iota(jnp.int32, (EDGE_ROWS, LANES), 1)
    first = jnp.zeros((EDGE_ROWS, LANES), jnp.float32)
    last = jnp.zeros((EDGE_ROWS, LANES), jnp.float32)
    for s in range(nspec):
        here = cells[s]
        first = jnp.where(lane == s, pltpu.roll(here, s, 1), first)
        last = jnp.where(lane == s, pltpu.roll(here, s + 1, 1), last)
    first_col[...] = first
    last_col[...] = last

    @pl.when(step == 0)
    def _():
        first_row[...] = cells[:, 0, :]

    @pl.when(step == pl.num_programs(0) - 1)
    def _():
        last_row[...] = cells[:, EDGE_ROWS - 1, :]


def matrices_kernel(nspec, pad, prop, lhs, rows):
    width = nspec * nspec
    lane = lax.broadcasted_iota(jnp.int32, (PREP_ROWS, LANES), 1)

    def window(start):
        if start + LANES <= width:
            return prop[:, start : start + LANES]
        tail = prop[:, start:width]
        return jnp.concatenate([tail, jnp.zeros((PREP_ROWS, start + LANES - width), jnp.float32)], axis=1)

    for i in range(nspec, pad):
        rows[pl.ds(i, PREP_ROWS, stride=pad), :] = jnp.zeros((PREP_ROWS, LANES), jnp.float32)
    for i in range(nspec):
        start = i * nspec // LANES * LANES
        skip = i * nspec - start
        piece = window(start)
        if skip:
            piece = pltpu.roll(piece, LANES - skip, 1)
        if skip + nspec > LANES:
            piece = jnp.where(lane < LANES - skip, piece, pltpu.roll(window(start + LANES), LANES - skip, 1))
        rows[pl.ds(i, PREP_ROWS, stride=pad), :] = jnp.where(lane < nspec, piece, 0.0)
    for g in range(PREP_ROWS):
        mat = rows[g * pad : (g + 1) * pad, :]
        high = mat.astype(jnp.bfloat16).astype(jnp.float32)
        both = jnp.concatenate([high, mat - high], axis=0)
        both = both + pltpu.roll(both, LANES // 2, 1)
        k = g % 2
        lhs[g // 2, :, k * LANES : (k + 1) * LANES] = both.astype(jnp.bfloat16)


def react_kernel(nspec, pad, counts, coef, cells, top, bottom, left, right, lhs, rate, out, state):
    rows_total = cells.shape[1]
    base = pl.program_id(0) * GROUP
    lane = lax.broadcasted_iota(jnp.int32, (GROUP, LANES), 1)
    sub = lax.broadcasted_iota(jnp.int32, (GROUP, LANES), 0)
    at_top = base == 0
    at_bottom = base + GROUP == rows_total
    row_above = jnp.maximum(base - 1, 0)
    row_below = jnp.minimum(base + GROUP, rows_total - 1)
    left_cols = left[pl.ds(base, GROUP), :]
    right_cols = right[pl.ds(base, GROUP), :]

    for s in range(nspec, pad):
        state[pl.ds(s, GROUP, stride=pad), :] = jnp.zeros((GROUP, LANES), jnp.float32)
    for s in range(nspec):
        here = cells[s, pl.ds(base, GROUP), :]
        before = jnp.where(at_top, top[s : s + 1, :], cells[s, pl.ds(row_above, 1), :])
        after = jnp.where(at_bottom, bottom[s : s + 1, :], cells[s, pl.ds(row_below, 1), :])
        above = jnp.where(sub == 0, before, pltpu.roll(here, 1, 0))
        below = jnp.where(sub == GROUP - 1, after, pltpu.roll(here, GROUP - 1, 0))
        edge_l = pltpu.roll(left_cols, LANES - 1 - s, 1)
        edge_r = pltpu.roll(right_cols, (LANES - s) % LANES, 1) if s else right_cols
        from_l = pltpu.roll(jnp.where(lane == LANES - 1, edge_l, here), 1, 1)
        from_r = pltpu.roll(jnp.where(lane == 0, edge_r, here), LANES - 1, 1)
        moved = here + coef[s] * ((above + below) + (from_l + from_r) - 4.0 * here)
        state[pl.ds(s, GROUP, stride=pad), :] = moved

    most = counts[base]
    for g in range(1, GROUP):
        most = jnp.maximum(most, counts[base + g])

    tail_rows = jnp.zeros((LANES // 2 - pad, LANES), jnp.float32)
    nothing = jnp.zeros((LANES, LANES), jnp.bfloat16)

    def parts(g):
        now = state[g * pad : (g + 1) * pad, :]
        pushed = now + rate[g : g + 1, :] * jnp.tanh(now)
        full = jnp.concatenate([pushed, tail_rows], axis=0)
        high = full.astype(jnp.bfloat16)
        low = (full - high.astype(jnp.float32)).astype(jnp.bfloat16)
        return jnp.concatenate([high, low], axis=0)

    def substep(step):
        for p in range(GROUP // 2):
            rhs = jnp.concatenate(
                [
                    jnp.concatenate([parts(2 * p), nothing], axis=1),
                    jnp.concatenate([nothing, parts(2 * p + 1)], axis=1),
                ],
                axis=0,
            )
            sums = jnp.dot(lhs[p], rhs, preferred_element_type=jnp.float32)
            sums = sums[0:pad] + sums[pad : 2 * pad]
            for k in range(2):
                g = 2 * p + k
                mask = jnp.broadcast_to(step < counts[base + g], (pad, LANES))
                pltpu.store(state.at[pl.ds(g * pad, pad), :], sums[:, k * LANES : (k + 1) * LANES], mask=mask)

    def several(i, carry):
        for u in range(UNROLL):
            substep(i * UNROLL + u)
        return carry

    def single(i, carry):
        substep(i)
        return carry

    whole = most // UNROLL
    lax.fori_loop(0, whole, several, 0)
    lax.fori_loop(whole * UNROLL, most, single, 0)

    for s in range(nspec):
        out[s] = state[pl.ds(s, GROUP, stride=pad), :]


def body(species, diffusivity, propagator, reaction_rate, substeps):
    rows, nspec, lanes = species.shape
    pad = (nspec + 7) // 8 * 8
    f32 = jnp.float32
    cells = species.transpose(1, 0, 2)

    def shift(values, axis, up):
        count = lax.axis_size(axis)
        pairs = [(i, (i + 1) % count) if up else ((i + 1) % count, i) for i in range(count)]
        return lax.ppermute(values, axis, pairs)

    first_col, last_col, first_row, last_row = pl.pallas_call(
        functools.partial(edges_kernel, nspec),
        name="edges",
        grid=(rows // EDGE_ROWS,),
        in_specs=[pl.BlockSpec((nspec, EDGE_ROWS, lanes), lambda i: (0, i, 0))],
        out_specs=[
            pl.BlockSpec((EDGE_ROWS, lanes), lambda i: (i, 0)),
            pl.BlockSpec((EDGE_ROWS, lanes), lambda i: (i, 0)),
            pl.BlockSpec((nspec, lanes), lambda i: (0, 0)),
            pl.BlockSpec((nspec, lanes), lambda i: (0, 0)),
        ],
        out_shape=[jax.ShapeDtypeStruct((rows, lanes), f32)] * 2 + [jax.ShapeDtypeStruct((nspec, lanes), f32)] * 2,
        compiler_params=pltpu.CompilerParams(vmem_limit_bytes=8 << 20),
        cost_estimate=pl.CostEstimate(flops=1 << 20, bytes_accessed=4 << 20, transcendentals=0),
    )(cells)

    top = shift(last_row, "space", True)
    bottom = shift(first_row, "space", False)
    left = shift(last_col, "pencil", True)
    right = shift(first_col, "pencil", False)

    lhs = pl.pallas_call(
        functools.partial(matrices_kernel, nspec, pad),
        name="matrices",
        grid=(rows // PREP_ROWS,),
        in_specs=[pl.BlockSpec((PREP_ROWS, nspec * nspec), lambda i: (i, 0))],
        out_specs=pl.BlockSpec((PREP_ROWS // 2, 2 * pad, 2 * lanes), lambda i: (i, 0, 0)),
        out_shape=jax.ShapeDtypeStruct((rows // 2, 2 * pad, 2 * lanes), jnp.bfloat16),
        scratch_shapes=[pltpu.VMEM((PREP_ROWS * pad, lanes), f32)],
        compiler_params=pltpu.CompilerParams(vmem_limit_bytes=8 << 20),
        cost_estimate=pl.CostEstimate(flops=1 << 24, bytes_accessed=6 << 20, transcendentals=0),
    )(propagator)

    once = pl.Buffered(1)
    result = pl.pallas_call(
        functools.partial(react_kernel, nspec, pad),
        name="react",
        out_shape=jax.ShapeDtypeStruct((nspec, rows, lanes), f32),
        grid_spec=pltpu.PrefetchScalarGridSpec(
            num_scalar_prefetch=2,
            grid=(rows // GROUP,),
            in_specs=[
                pl.BlockSpec((nspec, rows, lanes), lambda i, c, d: (0, 0, 0), pipeline_mode=once),
                pl.BlockSpec((nspec, lanes), lambda i, c, d: (0, 0), pipeline_mode=once),
                pl.BlockSpec((nspec, lanes), lambda i, c, d: (0, 0), pipeline_mode=once),
                pl.BlockSpec((rows, lanes), lambda i, c, d: (0, 0), pipeline_mode=once),
                pl.BlockSpec((rows, lanes), lambda i, c, d: (0, 0), pipeline_mode=once),
                pl.BlockSpec((GROUP // 2, 2 * pad, 2 * lanes), lambda i, c, d: (i, 0, 0)),
                pl.BlockSpec((GROUP, lanes), lambda i, c, d: (i, 0)),
            ],
            out_specs=pl.BlockSpec((nspec, GROUP, lanes), lambda i, c, d: (0, i, 0)),
            scratch_shapes=[pltpu.VMEM((GROUP * pad, lanes), f32)],
        ),
        compiler_params=pltpu.CompilerParams(vmem_limit_bytes=24 << 20),
        cost_estimate=pl.CostEstimate(flops=20 * rows * 2 * pad * 256 * 256, bytes_accessed=9 << 20, transcendentals=0),
    )(substeps.reshape(rows), diffusivity, cells, top, bottom, left, right, lhs, reaction_rate)
    return result.transpose(1, 0, 2)


def solution(mesh):
    return jax.shard_map(
        body,
        mesh=mesh,
        in_specs=(
            P("space", None, "pencil"),
            P(),
            P("space", "pencil"),
            P("space", "pencil"),
            P("space", "pencil"),
        ),
        out_specs=P("space", None, "pencil"),
        check_vma=False,
    )
```

```python
import functools

import jax
import jax.numpy as jnp
from jax import lax
from jax.experimental import pallas as pl
from jax.experimental.pallas import tpu as pltpu
from jax.sharding import PartitionSpec as P

CHUNKS = 6
PREP_ROWS = 16
GROUP = 32
UNROLLS = (8, 4, 2, 1)
LANES = 128


def edges_kernel(nspec, source, cells, cols, first_row, last_row, sems):
    rows = cells.shape[1]
    cuts = [nspec * k // CHUNKS for k in range(CHUNKS + 1)]
    copies = []
    for k in range(CHUNKS):
        part = pl.ds(cuts[k], cuts[k + 1] - cuts[k])
        copies.append(pltpu.make_async_copy(source.at[part], cells.at[part], sems.at[k]))
        copies[-1].start()
    lane = lax.broadcasted_iota(jnp.int32, (8, LANES), 1)
    for k in range(CHUNKS):
        copies[k].wait()
        picks = [(lane == 2 * s) | (lane == (2 * s - 1) % LANES) for s in range(cuts[k], cuts[k + 1])]
        for r in range(0, rows, 8):
            held = jnp.zeros((8, LANES), jnp.float32) if k == 0 else cols[r : r + 8, :]
            for pick, s in zip(picks, range(cuts[k], cuts[k + 1])):
                here = cells[s, r : r + 8, :]
                held = jnp.where(pick, pltpu.roll(here, 2 * s, 1) if s else here, held)
            cols[r : r + 8, :] = held
    first_row[...] = cells[:, 0, :]
    last_row[...] = cells[:, rows - 1, :]


def matrices_kernel(nspec, pad, prop, lhs, rows):
    width = nspec * nspec
    half = LANES // 2
    lane = lax.broadcasted_iota(jnp.int32, (PREP_ROWS, LANES), 1)

    def window(start):
        if start + LANES <= width:
            return prop[:, start : start + LANES]
        tail = prop[:, start:width]
        return jnp.concatenate([tail, jnp.zeros((PREP_ROWS, start + LANES - width), jnp.float32)], axis=1)

    for i in range(nspec, pad):
        rows[pl.ds(i, PREP_ROWS, stride=pad), :] = jnp.zeros((PREP_ROWS, LANES), jnp.float32)
    for i in range(nspec):
        start = i * nspec // LANES * LANES
        skip = i * nspec - start
        piece = window(start)
        if skip + nspec > LANES:
            piece = jnp.where(lane >= skip, piece, window(start + LANES))
        once = pltpu.roll(piece, LANES - skip, 1) if skip else piece
        again = pltpu.roll(piece, (half - skip) % LANES, 1) if skip != half else piece
        twice = jnp.where(lane < nspec, once, jnp.where((lane >= half) & (lane < half + nspec), again, 0.0))
        rows[pl.ds(i, PREP_ROWS, stride=pad), :] = twice
    for g in range(PREP_ROWS):
        mat = rows[g * pad : (g + 1) * pad, :]
        high = mat.astype(jnp.bfloat16).astype(jnp.float32)
        both = jnp.concatenate([high, mat - high], axis=0)
        k = g % 2
        lhs[g // 2, :, k * LANES : (k + 1) * LANES] = both.astype(jnp.bfloat16)


def react_kernel(nspec, pad, counts, coef, cells, top, bottom, left, right, lhs, rate, out, state):
    rows_total = cells.shape[1]
    base = pl.program_id(0) * GROUP
    lane = lax.broadcasted_iota(jnp.int32, (GROUP, LANES), 1)
    sub = lax.broadcasted_iota(jnp.int32, (GROUP, LANES), 0)
    at_top = base == 0
    at_bottom = base + GROUP == rows_total
    row_above = jnp.maximum(base - 1, 0)
    row_below = jnp.minimum(base + GROUP, rows_total - 1)
    edge_cols = jnp.where(
        lane % 2 == 0,
        pltpu.roll(left[pl.ds(base, GROUP), :], 1, 1),
        pltpu.roll(right[pl.ds(base, GROUP), :], LANES - 1, 1),
    )

    for s in range(nspec, pad):
        state[pl.ds(s, GROUP, stride=pad), :] = jnp.zeros((GROUP, LANES), jnp.float32)
    for s in range(nspec):
        here = cells[s, pl.ds(base, GROUP), :]
        before = jnp.where(at_top, top[s : s + 1, :], cells[s, pl.ds(row_above, 1), :])
        after = jnp.where(at_bottom, bottom[s : s + 1, :], cells[s, pl.ds(row_below, 1), :])
        above = jnp.where(sub == 0, before, pltpu.roll(here, 1, 0))
        below = jnp.where(sub == GROUP - 1, after, pltpu.roll(here, GROUP - 1, 0))
        edge = pltpu.roll(edge_cols, LANES - 2 * s, 1) if s else edge_cols
        from_l = jnp.where(lane == 0, edge, pltpu.roll(here, 1, 1))
        from_r = jnp.where(lane == LANES - 1, edge, pltpu.roll(here, LANES - 1, 1))
        moved = here + coef[s] * ((above + below) + (from_l + from_r) - 4.0 * here)
        state[pl.ds(s, GROUP, stride=pad), :] = moved

    most = counts[base]
    for g in range(1, GROUP):
        most = jnp.maximum(most, counts[base + g])

    tail_rows = jnp.zeros((LANES // 2 - pad, LANES), jnp.float32)
    nothing = jnp.zeros((LANES, LANES), jnp.bfloat16)

    def parts(g):
        now = state[g * pad : (g + 1) * pad, :]
        pushed = now + rate[g : g + 1, :] * jnp.tanh(now)
        full = jnp.concatenate([pushed, tail_rows], axis=0)
        high = full.astype(jnp.bfloat16)
        low = (full - high.astype(jnp.float32)).astype(jnp.bfloat16)
        return jnp.concatenate([high, low], axis=0)

    def substep(step):
        for p in range(GROUP // 2):
            rhs = jnp.concatenate(
                [
                    jnp.concatenate([parts(2 * p), nothing], axis=1),
                    jnp.concatenate([nothing, parts(2 * p + 1)], axis=1),
                ],
                axis=0,
            )
            sums = jnp.dot(lhs[p], rhs, preferred_element_type=jnp.float32)
            sums = sums[0:pad] + sums[pad : 2 * pad]
            for k in range(2):
                g = 2 * p + k
                mask = jnp.broadcast_to(step < counts[base + g], (pad, LANES))
                pltpu.store(state.at[pl.ds(g * pad, pad), :], sums[:, k * LANES : (k + 1) * LANES], mask=mask)

    def run(count, start):
        def steps(i, step):
            for u in range(count):
                substep(step + u)
            return step + count

        return lax.fori_loop(0, (most - start) // count, steps, start)

    done = 0
    for count in UNROLLS:
        done = run(count, done)

    for s in range(nspec):
        out[s] = state[pl.ds(s, GROUP, stride=pad), :]


def body(species, diffusivity, propagator, reaction_rate, substeps):
    rows, nspec, lanes = species.shape
    pad = (nspec + 7) // 8 * 8
    f32 = jnp.float32
    cells = species.transpose(1, 0, 2)

    def shift(values, axis, up):
        count = lax.axis_size(axis)
        pairs = [(i, (i + 1) % count) if up else ((i + 1) % count, i) for i in range(count)]
        return lax.ppermute(values, axis, pairs)

    whole = pl.BlockSpec(memory_space=pltpu.VMEM)
    near, cols, first_row, last_row = pl.pallas_call(
        functools.partial(edges_kernel, nspec),
        name="edges",
        in_specs=[pl.BlockSpec(memory_space=pltpu.HBM)],
        out_specs=[whole] * 4,
        out_shape=[jax.ShapeDtypeStruct((nspec, rows, lanes), f32), jax.ShapeDtypeStruct((rows, lanes), f32)]
        + [jax.ShapeDtypeStruct((nspec, lanes), f32)] * 2,
        scratch_shapes=[pltpu.SemaphoreType.DMA((CHUNKS,))],
        compiler_params=pltpu.CompilerParams(vmem_limit_bytes=8 << 20),
        cost_estimate=pl.CostEstimate(flops=1 << 20, bytes_accessed=4 << 20, transcendentals=0),
    )(pltpu.with_memory_space_constraint(cells, pltpu.HBM))

    left = shift(cols, "pencil", True)
    right = shift(cols, "pencil", False)
    top = shift(last_row, "space", True)
    bottom = shift(first_row, "space", False)

    lhs = pl.pallas_call(
        functools.partial(matrices_kernel, nspec, pad),
        name="matrices",
        grid=(rows // PREP_ROWS,),
        in_specs=[pl.BlockSpec((PREP_ROWS, nspec * nspec), lambda i: (i, 0))],
        out_specs=pl.BlockSpec((PREP_ROWS // 2, 2 * pad, 2 * lanes), lambda i: (i, 0, 0)),
        out_shape=jax.ShapeDtypeStruct((rows // 2, 2 * pad, 2 * lanes), jnp.bfloat16),
        scratch_shapes=[pltpu.VMEM((PREP_ROWS * pad, lanes), f32)],
        compiler_params=pltpu.CompilerParams(vmem_limit_bytes=8 << 20),
        cost_estimate=pl.CostEstimate(flops=1 << 24, bytes_accessed=6 << 20, transcendentals=0),
    )(propagator)

    once = pl.Buffered(1)
    result = pl.pallas_call(
        functools.partial(react_kernel, nspec, pad),
        name="react",
        out_shape=jax.ShapeDtypeStruct((nspec, rows, lanes), f32),
        grid_spec=pltpu.PrefetchScalarGridSpec(
            num_scalar_prefetch=2,
            grid=(rows // GROUP,),
            in_specs=[
                pl.BlockSpec((nspec, rows, lanes), lambda i, c, d: (0, 0, 0), pipeline_mode=once),
                pl.BlockSpec((nspec, lanes), lambda i, c, d: (0, 0), pipeline_mode=once),
                pl.BlockSpec((nspec, lanes), lambda i, c, d: (0, 0), pipeline_mode=once),
                pl.BlockSpec((rows, lanes), lambda i, c, d: (0, 0), pipeline_mode=once),
                pl.BlockSpec((rows, lanes), lambda i, c, d: (0, 0), pipeline_mode=once),
                pl.BlockSpec((GROUP // 2, 2 * pad, 2 * lanes), lambda i, c, d: (i, 0, 0)),
                pl.BlockSpec((GROUP, lanes), lambda i, c, d: (i, 0)),
            ],
            out_specs=pl.BlockSpec((nspec, GROUP, lanes), lambda i, c, d: (0, i, 0)),
            scratch_shapes=[pltpu.VMEM((GROUP * pad, lanes), f32)],
        ),
        compiler_params=pltpu.CompilerParams(vmem_limit_bytes=24 << 20),
        cost_estimate=pl.CostEstimate(flops=20 * rows * 2 * pad * 256 * 256, bytes_accessed=9 << 20, transcendentals=0),
    )(substeps.reshape(rows), diffusivity, near, top, bottom, left, right, lhs, reaction_rate)
    return result.transpose(1, 0, 2)


def solution(mesh):
    return jax.shard_map(
        body,
        mesh=mesh,
        in_specs=(
            P("space", None, "pencil"),
            P(),
            P("space", "pencil"),
            P("space", "pencil"),
            P("space", "pencil"),
        ),
        out_specs=P("space", None, "pencil"),
        check_vma=False,
    )
```

```python
import functools

import jax
import jax.numpy as jnp
from jax import lax
from jax.experimental import pallas as pl
from jax.experimental.pallas import tpu as pltpu
from jax.sharding import PartitionSpec as P

CHUNKS = 6
PREP_ROWS = 16
GROUP = 32
LAG = 8
UNROLLS = (12, 6, 3, 2, 1)
LANES = 128


def edges_kernel(nspec, source, cells, cols, first_row, last_row, sems):
    rows = cells.shape[1]
    cuts = [nspec * k // CHUNKS for k in range(CHUNKS + 1)]
    copies = []
    for k in range(CHUNKS):
        part = pl.ds(cuts[k], cuts[k + 1] - cuts[k])
        copies.append(pltpu.make_async_copy(source.at[part], cells.at[part], sems.at[k]))
        copies[-1].start()
    lane = lax.broadcasted_iota(jnp.int32, (8, LANES), 1)
    for k in range(CHUNKS):
        copies[k].wait()
        picks = [(lane == 2 * s) | (lane == (2 * s - 1) % LANES) for s in range(cuts[k], cuts[k + 1])]
        for r in range(0, rows, 8):
            held = jnp.zeros((8, LANES), jnp.float32) if k == 0 else cols[r : r + 8, :]
            for pick, s in zip(picks, range(cuts[k], cuts[k + 1])):
                here = cells[s, r : r + 8, :]
                held = jnp.where(pick, pltpu.roll(here, 2 * s, 1) if s else here, held)
            cols[r : r + 8, :] = held
    first_row[...] = cells[:, 0, :]
    last_row[...] = cells[:, rows - 1, :]


def matrices_kernel(nspec, pad, prop, lhs, rows):
    width = nspec * nspec
    half = LANES // 2
    lane = lax.broadcasted_iota(jnp.int32, (PREP_ROWS, LANES), 1)

    def window(start):
        if start + LANES <= width:
            return prop[:, start : start + LANES]
        tail = prop[:, start:width]
        return jnp.concatenate([tail, jnp.zeros((PREP_ROWS, start + LANES - width), jnp.float32)], axis=1)

    for i in range(nspec, pad):
        rows[pl.ds(i, PREP_ROWS, stride=pad), :] = jnp.zeros((PREP_ROWS, LANES), jnp.float32)
    for i in range(nspec):
        start = i * nspec // LANES * LANES
        skip = i * nspec - start
        piece = window(start)
        if skip + nspec > LANES:
            piece = jnp.where(lane >= skip, piece, window(start + LANES))
        once = pltpu.roll(piece, LANES - skip, 1) if skip else piece
        again = pltpu.roll(piece, (half - skip) % LANES, 1) if skip != half else piece
        twice = jnp.where(lane < nspec, once, jnp.where((lane >= half) & (lane < half + nspec), again, 0.0))
        rows[pl.ds(i, PREP_ROWS, stride=pad), :] = twice
    for g in range(PREP_ROWS):
        mat = rows[g * pad : (g + 1) * pad, :]
        high = mat.astype(jnp.bfloat16).astype(jnp.float32)
        both = jnp.concatenate([high, mat - high], axis=0)
        k = g % 2
        lhs[g // 2, :, k * LANES : (k + 1) * LANES] = both.astype(jnp.bfloat16)


def react_kernel(nspec, pad, counts, coef, cells, top, bottom, left, right, lhs, rate, out, state):
    pl.run_scoped(
        functools.partial(react_group, nspec, pad, counts, coef, cells, top, bottom, left, right, lhs, rate, out, state),
        *[pltpu.ACC(mxu_id=p % 2)((2 * pad, 2 * LANES), jnp.float32) for p in range(GROUP // 2)],
    )


def react_group(nspec, pad, counts, coef, cells, top, bottom, left, right, lhs, rate, out, state, *sums):
    rows_total = cells.shape[1]
    base = pl.program_id(0) * GROUP
    lane = lax.broadcasted_iota(jnp.int32, (GROUP, LANES), 1)
    sub = lax.broadcasted_iota(jnp.int32, (GROUP, LANES), 0)
    at_top = base == 0
    at_bottom = base + GROUP == rows_total
    row_above = jnp.maximum(base - 1, 0)
    row_below = jnp.minimum(base + GROUP, rows_total - 1)
    edge_cols = jnp.where(
        lane % 2 == 0,
        pltpu.roll(left[pl.ds(base, GROUP), :], 1, 1),
        pltpu.roll(right[pl.ds(base, GROUP), :], LANES - 1, 1),
    )

    for s in range(nspec, pad):
        state[pl.ds(s, GROUP, stride=pad), :] = jnp.zeros((GROUP, LANES), jnp.float32)
    for s in range(nspec):
        here = cells[s, pl.ds(base, GROUP), :]
        before = jnp.where(at_top, top[s : s + 1, :], cells[s, pl.ds(row_above, 1), :])
        after = jnp.where(at_bottom, bottom[s : s + 1, :], cells[s, pl.ds(row_below, 1), :])
        above = jnp.where(sub == 0, before, pltpu.roll(here, 1, 0))
        below = jnp.where(sub == GROUP - 1, after, pltpu.roll(here, GROUP - 1, 0))
        edge = pltpu.roll(edge_cols, LANES - 2 * s, 1) if s else edge_cols
        from_l = jnp.where(lane == 0, edge, pltpu.roll(here, 1, 1))
        from_r = jnp.where(lane == LANES - 1, edge, pltpu.roll(here, LANES - 1, 1))
        moved = here + coef[s] * ((above + below) + (from_l + from_r) - 4.0 * here)
        state[pl.ds(s, GROUP, stride=pad), :] = moved

    most = counts[base]
    for g in range(1, GROUP):
        most = jnp.maximum(most, counts[base + g])

    tail_rows = jnp.zeros((LANES // 2 - pad, LANES), jnp.float32)
    nothing = jnp.zeros((LANES, LANES), jnp.bfloat16)

    def parts(g):
        now = state[g * pad : (g + 1) * pad, :]
        pushed = now + rate[g : g + 1, :] * jnp.tanh(now)
        full = jnp.concatenate([pushed, tail_rows], axis=0)
        high = full.astype(jnp.bfloat16)
        low = (full - high.astype(jnp.float32)).astype(jnp.bfloat16)
        return jnp.concatenate([high, low], axis=0)

    pairs = GROUP // 2

    def launch(p):
        rhs = jnp.concatenate(
            [
                jnp.concatenate([parts(2 * p), nothing], axis=1),
                jnp.concatenate([nothing, parts(2 * p + 1)], axis=1),
            ],
            axis=0,
        )
        slot = p // 2 % 2
        pltpu.matmul_push_rhs(rhs, slot, p % 2)
        pltpu.matmul_acc_lhs(sums[p], lhs[p], load_staged_rhs=slot)

    def take(p, step):
        both = pltpu.matmul_pop(sums[p])
        fresh = both[0:pad] + both[pad : 2 * pad]
        for k in range(2):
            g = 2 * p + k
            mask = jnp.broadcast_to(step < counts[base + g], (pad, LANES))
            pltpu.store(state.at[pl.ds(g * pad, pad), :], fresh[:, k * LANES : (k + 1) * LANES], mask=mask)

    for p in range(pairs):
        launch(p)
        if p >= LAG:
            take(p - LAG, 0)

    def substep(step):
        for p in range(pairs):
            launch(p)
            if p >= LAG:
                take(p - LAG, step)
            else:
                take(pairs - LAG + p, step - 1)

    done = 1
    for count in UNROLLS:

        def several(i, step, count=count):
            for u in range(count):
                substep(step + u)
            return step + count

        done = lax.fori_loop(0, (most - done) // count, several, done)
    for p in range(pairs - LAG, pairs):
        take(p, most - 1)

    for s in range(nspec):
        out[s] = state[pl.ds(s, GROUP, stride=pad), :]


def body(species, diffusivity, propagator, reaction_rate, substeps):
    rows, nspec, lanes = species.shape
    pad = (nspec + 7) // 8 * 8
    f32 = jnp.float32
    cells = species.transpose(1, 0, 2)

    def shift(values, axis, up):
        count = lax.axis_size(axis)
        pairs = [(i, (i + 1) % count) if up else ((i + 1) % count, i) for i in range(count)]
        return lax.ppermute(values, axis, pairs)

    whole = pl.BlockSpec(memory_space=pltpu.VMEM)
    near, cols, first_row, last_row = pl.pallas_call(
        functools.partial(edges_kernel, nspec),
        name="edges",
        in_specs=[pl.BlockSpec(memory_space=pltpu.HBM)],
        out_specs=[whole] * 4,
        out_shape=[jax.ShapeDtypeStruct((nspec, rows, lanes), f32), jax.ShapeDtypeStruct((rows, lanes), f32)]
        + [jax.ShapeDtypeStruct((nspec, lanes), f32)] * 2,
        scratch_shapes=[pltpu.SemaphoreType.DMA((CHUNKS,))],
        compiler_params=pltpu.CompilerParams(vmem_limit_bytes=8 << 20),
        cost_estimate=pl.CostEstimate(flops=1 << 20, bytes_accessed=4 << 20, transcendentals=0),
    )(pltpu.with_memory_space_constraint(cells, pltpu.HBM))

    left = shift(cols, "pencil", True)
    right = shift(cols, "pencil", False)
    top = shift(last_row, "space", True)
    bottom = shift(first_row, "space", False)

    lhs = pl.pallas_call(
        functools.partial(matrices_kernel, nspec, pad),
        name="matrices",
        grid=(rows // PREP_ROWS,),
        in_specs=[pl.BlockSpec((PREP_ROWS, nspec * nspec), lambda i: (i, 0))],
        out_specs=pl.BlockSpec((PREP_ROWS // 2, 2 * pad, 2 * lanes), lambda i: (i, 0, 0)),
        out_shape=jax.ShapeDtypeStruct((rows // 2, 2 * pad, 2 * lanes), jnp.bfloat16),
        scratch_shapes=[pltpu.VMEM((PREP_ROWS * pad, lanes), f32)],
        compiler_params=pltpu.CompilerParams(vmem_limit_bytes=8 << 20),
        cost_estimate=pl.CostEstimate(flops=1 << 24, bytes_accessed=6 << 20, transcendentals=0),
    )(propagator)

    once = pl.Buffered(1)
    result = pl.pallas_call(
        functools.partial(react_kernel, nspec, pad),
        name="react",
        out_shape=jax.ShapeDtypeStruct((nspec, rows, lanes), f32),
        grid_spec=pltpu.PrefetchScalarGridSpec(
            num_scalar_prefetch=2,
            grid=(rows // GROUP,),
            in_specs=[
                pl.BlockSpec((nspec, rows, lanes), lambda i, c, d: (0, 0, 0), pipeline_mode=once),
                pl.BlockSpec((nspec, lanes), lambda i, c, d: (0, 0), pipeline_mode=once),
                pl.BlockSpec((nspec, lanes), lambda i, c, d: (0, 0), pipeline_mode=once),
                pl.BlockSpec((rows, lanes), lambda i, c, d: (0, 0), pipeline_mode=once),
                pl.BlockSpec((rows, lanes), lambda i, c, d: (0, 0), pipeline_mode=once),
                pl.BlockSpec((GROUP // 2, 2 * pad, 2 * lanes), lambda i, c, d: (i, 0, 0)),
                pl.BlockSpec((GROUP, lanes), lambda i, c, d: (i, 0)),
            ],
            out_specs=pl.BlockSpec((nspec, GROUP, lanes), lambda i, c, d: (0, i, 0)),
            scratch_shapes=[pltpu.VMEM((GROUP * pad, lanes), f32)],
        ),
        compiler_params=pltpu.CompilerParams(vmem_limit_bytes=24 << 20),
        cost_estimate=pl.CostEstimate(flops=20 * rows * 2 * pad * 256 * 256, bytes_accessed=9 << 20, transcendentals=0),
    )(substeps.reshape(rows), diffusivity, near, top, bottom, left, right, lhs, reaction_rate)
    return result.transpose(1, 0, 2)


def solution(mesh):
    def whole(*args):
        with jax.sharding.use_abstract_mesh(mesh.abstract_mesh):
            return mapped(*args)

    mapped = jax.shard_map(
        body,
        mesh=mesh,
        in_specs=(
            P("space", None, "pencil"),
            P(),
            P("space", "pencil"),
            P("space", "pencil"),
            P("space", "pencil"),
        ),
        out_specs=P("space", None, "pencil"),
        check_vma=False,
    )
    return whole
```

```python
import functools

import jax
import jax.numpy as jnp
from jax import lax
from jax.experimental import pallas as pl
from jax.experimental.pallas import tpu as pltpu
from jax.sharding import PartitionSpec as P

CHUNKS = 6
PREP_ROWS = 16
GROUP = 32
UNROLLS = (14, 7, 4, 2, 1)
LANES = 128


def edges_kernel(nspec, source, cells, cols, first_row, last_row, sems):
    rows = cells.shape[1]
    cuts = [nspec * k // CHUNKS for k in range(CHUNKS + 1)]
    copies = []
    for k in range(CHUNKS):
        part = pl.ds(cuts[k], cuts[k + 1] - cuts[k])
        copies.append(pltpu.make_async_copy(source.at[part], cells.at[part], sems.at[k]))
        copies[-1].start()
    lane = lax.broadcasted_iota(jnp.int32, (8, LANES), 1)
    for k in range(CHUNKS):
        copies[k].wait()
        picks = [(lane == 2 * s) | (lane == (2 * s - 1) % LANES) for s in range(cuts[k], cuts[k + 1])]
        for r in range(0, rows, 8):
            held = jnp.zeros((8, LANES), jnp.float32) if k == 0 else cols[r : r + 8, :]
            for pick, s in zip(picks, range(cuts[k], cuts[k + 1])):
                here = cells[s, r : r + 8, :]
                held = jnp.where(pick, pltpu.roll(here, 2 * s, 1) if s else here, held)
            cols[r : r + 8, :] = held
    first_row[...] = cells[:, 0, :]
    last_row[...] = cells[:, rows - 1, :]


def matrices_kernel(nspec, pad, prop, lhs, rows):
    width = nspec * nspec
    lane = lax.broadcasted_iota(jnp.int32, (8, LANES), 1)

    def window(part, start):
        if start + LANES <= width:
            return prop[part, start : start + LANES]
        tail = prop[part, start:width]
        return jnp.concatenate([tail, jnp.zeros((8, start + LANES - width), jnp.float32)], axis=1)

    for i in range(nspec, pad):
        rows[pl.ds(i, PREP_ROWS, stride=pad), :] = jnp.zeros((PREP_ROWS, LANES), jnp.float32)
    for i in range(nspec):
        start = i * nspec // LANES * LANES
        skip = i * nspec - start
        for k in range(2):
            part = slice(8 * k, 8 * k + 8)
            piece = window(part, start)
            if skip + nspec > LANES:
                piece = jnp.where(lane >= skip, piece, window(part, start + LANES))
            twice = jnp.zeros((8, LANES), jnp.float32)
            for copy in range(2):
                at = (2 * k + copy) * pad % LANES
                turn = (at - skip) % LANES
                inside = (lane - at) % LANES < nspec
                twice = jnp.where(inside, pltpu.roll(piece, turn, 1) if turn else piece, twice)
            rows[pl.ds(8 * k * pad + i, 8, stride=pad), :] = twice
    wide = lax.broadcasted_iota(jnp.int32, (2 * pad, LANES), 1)
    for p in range(PREP_ROWS // 2):
        both = []
        for k in range(2):
            mat = rows[(p + 8 * k) * pad : (p + 8 * k + 1) * pad, :]
            high = mat.astype(jnp.bfloat16).astype(jnp.float32)
            both.append(jnp.concatenate([high, mat - high], axis=0))
        lhs[p, :, 0:LANES] = jnp.where(wide < 2 * pad, both[0], both[1]).astype(jnp.bfloat16)
        lhs[p, :, LANES : 2 * LANES] = jnp.where(wide < 2 * pad, both[1], 0.0).astype(jnp.bfloat16)


def react_kernel(nspec, pad, counts, coef, cells, top, bottom, left, right, lhs, rate, out, state):
    rows_total = cells.shape[1]
    base = pl.program_id(0) * GROUP
    lane = lax.broadcasted_iota(jnp.int32, (GROUP, LANES), 1)
    sub = lax.broadcasted_iota(jnp.int32, (GROUP, LANES), 0)
    at_top = base == 0
    at_bottom = base + GROUP == rows_total
    row_above = jnp.maximum(base - 1, 0)
    row_below = jnp.minimum(base + GROUP, rows_total - 1)
    edge_cols = jnp.where(
        lane % 2 == 0,
        pltpu.roll(left[pl.ds(base, GROUP), :], 1, 1),
        pltpu.roll(right[pl.ds(base, GROUP), :], LANES - 1, 1),
    )

    for s in range(nspec, pad):
        state[pl.ds(s, GROUP, stride=pad), :] = jnp.zeros((GROUP, LANES), jnp.float32)
    for s in range(nspec):
        here = cells[s, pl.ds(base, GROUP), :]
        before = jnp.where(at_top, top[s : s + 1, :], cells[s, pl.ds(row_above, 1), :])
        after = jnp.where(at_bottom, bottom[s : s + 1, :], cells[s, pl.ds(row_below, 1), :])
        above = jnp.where(sub == 0, before, pltpu.roll(here, 1, 0))
        below = jnp.where(sub == GROUP - 1, after, pltpu.roll(here, GROUP - 1, 0))
        edge = pltpu.roll(edge_cols, LANES - 2 * s, 1) if s else edge_cols
        from_l = jnp.where(lane == 0, edge, pltpu.roll(here, 1, 1))
        from_r = jnp.where(lane == LANES - 1, edge, pltpu.roll(here, LANES - 1, 1))
        moved = here + coef[s] * ((above + below) + (from_l + from_r) - 4.0 * here)
        state[pl.ds(s, GROUP, stride=pad), :] = moved

    most = counts[base]
    for g in range(1, GROUP):
        most = jnp.maximum(most, counts[base + g])

    odd_rows = jnp.zeros((8, LANES), jnp.float32)
    nothing = jnp.zeros((2 * pad, LANES), jnp.bfloat16)
    unused = jnp.zeros((2 * LANES - 4 * pad, 2 * LANES), jnp.bfloat16)

    def parts(g):
        now = state[g * pad : (g + 1) * pad, :]
        pushed = now + rate[g : g + 1, :] * jnp.tanh(now)
        high = jnp.concatenate([pushed, odd_rows], axis=0).astype(jnp.bfloat16).astype(jnp.float32)[0:pad]
        return jnp.concatenate([high, pushed - high], axis=0).astype(jnp.bfloat16)

    def substep(step):
        for p in range(GROUP // 2):
            ends = (p // 8 * 16 + p % 8, p // 8 * 16 + p % 8 + 8)
            rhs = jnp.concatenate(
                [
                    jnp.concatenate([parts(ends[0]), nothing], axis=1),
                    jnp.concatenate([nothing, parts(ends[1])], axis=1),
                    unused,
                ],
                axis=0,
            )
            sums = jnp.dot(lhs[p], rhs, preferred_element_type=jnp.float32)
            sums = sums[0:pad] + sums[pad : 2 * pad]
            for k, g in enumerate(ends):
                mask = jnp.broadcast_to(step < counts[base + g], (pad, LANES))
                pltpu.store(state.at[pl.ds(g * pad, pad), :], sums[:, k * LANES : (k + 1) * LANES], mask=mask)

    def run(count, trips, start):
        def steps(i, step):
            for u in range(count):
                substep(step + u)
            return step + count

        return lax.fori_loop(0, trips, steps, start)

    done = run(15, jnp.maximum(most - 28, 0), 0)
    for count in UNROLLS:
        done = run(count, (most - done) // count, done)

    for s in range(nspec):
        out[s] = state[pl.ds(s, GROUP, stride=pad), :]


def body(species, diffusivity, propagator, reaction_rate, substeps):
    rows, nspec, lanes = species.shape
    pad = (nspec + 7) // 8 * 8
    f32 = jnp.float32
    cells = species.transpose(1, 0, 2)

    def shift(values, axis, up):
        count = lax.axis_size(axis)
        pairs = [(i, (i + 1) % count) if up else ((i + 1) % count, i) for i in range(count)]
        return lax.ppermute(values, axis, pairs)

    whole = pl.BlockSpec(memory_space=pltpu.VMEM)
    near, cols, first_row, last_row = pl.pallas_call(
        functools.partial(edges_kernel, nspec),
        name="edges",
        in_specs=[pl.BlockSpec(memory_space=pltpu.HBM)],
        out_specs=[whole] * 4,
        out_shape=[jax.ShapeDtypeStruct((nspec, rows, lanes), f32), jax.ShapeDtypeStruct((rows, lanes), f32)]
        + [jax.ShapeDtypeStruct((nspec, lanes), f32)] * 2,
        scratch_shapes=[pltpu.SemaphoreType.DMA((CHUNKS,))],
        compiler_params=pltpu.CompilerParams(vmem_limit_bytes=8 << 20),
        cost_estimate=pl.CostEstimate(flops=1 << 20, bytes_accessed=4 << 20, transcendentals=0),
    )(pltpu.with_memory_space_constraint(cells, pltpu.HBM))

    left = shift(cols, "pencil", True)
    right = shift(cols, "pencil", False)
    top = shift(last_row, "space", True)
    bottom = shift(first_row, "space", False)

    lhs = pl.pallas_call(
        functools.partial(matrices_kernel, nspec, pad),
        name="matrices",
        grid=(rows // PREP_ROWS,),
        in_specs=[pl.BlockSpec((PREP_ROWS, nspec * nspec), lambda i: (i, 0))],
        out_specs=pl.BlockSpec((PREP_ROWS // 2, 2 * pad, 2 * lanes), lambda i: (i, 0, 0)),
        out_shape=jax.ShapeDtypeStruct((rows // 2, 2 * pad, 2 * lanes), jnp.bfloat16),
        scratch_shapes=[pltpu.VMEM((PREP_ROWS * pad, lanes), f32)],
        compiler_params=pltpu.CompilerParams(vmem_limit_bytes=8 << 20),
        cost_estimate=pl.CostEstimate(flops=1 << 24, bytes_accessed=6 << 20, transcendentals=0),
    )(propagator)

    once = pl.Buffered(1)
    result = pl.pallas_call(
        functools.partial(react_kernel, nspec, pad),
        name="react",
        out_shape=jax.ShapeDtypeStruct((nspec, rows, lanes), f32),
        grid_spec=pltpu.PrefetchScalarGridSpec(
            num_scalar_prefetch=2,
            grid=(rows // GROUP,),
            in_specs=[
                pl.BlockSpec((nspec, rows, lanes), lambda i, c, d: (0, 0, 0), pipeline_mode=once),
                pl.BlockSpec((nspec, lanes), lambda i, c, d: (0, 0), pipeline_mode=once),
                pl.BlockSpec((nspec, lanes), lambda i, c, d: (0, 0), pipeline_mode=once),
                pl.BlockSpec((rows, lanes), lambda i, c, d: (0, 0), pipeline_mode=once),
                pl.BlockSpec((rows, lanes), lambda i, c, d: (0, 0), pipeline_mode=once),
                pl.BlockSpec((GROUP // 2, 2 * pad, 2 * lanes), lambda i, c, d: (i, 0, 0)),
                pl.BlockSpec((GROUP, lanes), lambda i, c, d: (i, 0)),
            ],
            out_specs=pl.BlockSpec((nspec, GROUP, lanes), lambda i, c, d: (0, i, 0)),
            scratch_shapes=[pltpu.VMEM((GROUP * pad, lanes), f32)],
        ),
        compiler_params=pltpu.CompilerParams(vmem_limit_bytes=24 << 20),
        cost_estimate=pl.CostEstimate(flops=20 * rows * 2 * pad * 256 * 256, bytes_accessed=9 << 20, transcendentals=0),
    )(substeps.reshape(rows), diffusivity, near, top, bottom, left, right, lhs, reaction_rate)
    return result.transpose(1, 0, 2)


def solution(mesh):
    return jax.shard_map(
        body,
        mesh=mesh,
        in_specs=(
            P("space", None, "pencil"),
            P(),
            P("space", "pencil"),
            P("space", "pencil"),
            P("space", "pencil"),
        ),
        out_specs=P("space", None, "pencil"),
        check_vma=False,
    )
```

```python
import functools

import jax
import jax.numpy as jnp
from jax import lax
from jax.experimental import pallas as pl
from jax.experimental.pallas import tpu as pltpu
from jax.sharding import PartitionSpec as P

CHUNKS = 6
PREP_ROWS = 16
GROUP = 32
UNROLLS = (14, 7, 4, 2, 1)
LANES = 128


def edges_kernel(nspec, source, cells, cols, first_row, last_row, sems):
    rows = cells.shape[1]
    cuts = [nspec * k // CHUNKS for k in range(CHUNKS + 1)]
    copies = []
    for k in range(CHUNKS):
        part = pl.ds(cuts[k], cuts[k + 1] - cuts[k])
        copies.append(pltpu.make_async_copy(source.at[part], cells.at[part], sems.at[k]))
        copies[-1].start()
    lane = lax.broadcasted_iota(jnp.int32, (8, LANES), 1)
    for k in range(CHUNKS):
        copies[k].wait()
        picks = [(lane == 2 * s) | (lane == (2 * s - 1) % LANES) for s in range(cuts[k], cuts[k + 1])]
        for r in range(0, rows, 8):
            held = jnp.zeros((8, LANES), jnp.float32) if k == 0 else cols[r : r + 8, :]
            for pick, s in zip(picks, range(cuts[k], cuts[k + 1])):
                here = cells[s, r : r + 8, :]
                held = jnp.where(pick, pltpu.roll(here, 2 * s, 1) if s else here, held)
            cols[r : r + 8, :] = held
    first_row[...] = cells[:, 0, :]
    last_row[...] = cells[:, rows - 1, :]


def matrices_kernel(nspec, pad, prop, lhs, rows):
    width = nspec * nspec
    lane = lax.broadcasted_iota(jnp.int32, (8, LANES), 1)

    def window(part, start):
        if start + LANES <= width:
            return prop[part, start : start + LANES]
        tail = prop[part, start:width]
        return jnp.concatenate([tail, jnp.zeros((8, start + LANES - width), jnp.float32)], axis=1)

    for i in range(nspec, pad):
        rows[pl.ds(i, PREP_ROWS, stride=pad), :] = jnp.zeros((PREP_ROWS, LANES), jnp.float32)
    for i in range(nspec):
        start = i * nspec // LANES * LANES
        skip = i * nspec - start
        for k in range(2):
            part = slice(8 * k, 8 * k + 8)
            piece = window(part, start)
            if skip + nspec > LANES:
                piece = jnp.where(lane >= skip, piece, window(part, start + LANES))
            twice = jnp.zeros((8, LANES), jnp.float32)
            for copy in range(2):
                at = (2 * k + copy) * pad % LANES
                turn = (at - skip) % LANES
                inside = (lane - at) % LANES < nspec
                twice = jnp.where(inside, pltpu.roll(piece, turn, 1) if turn else piece, twice)
            rows[pl.ds(8 * k * pad + i, 8, stride=pad), :] = twice
    wide = lax.broadcasted_iota(jnp.int32, (2 * pad, LANES), 1)
    for p in range(PREP_ROWS // 2):
        both = []
        for k in range(2):
            mat = rows[(p + 8 * k) * pad : (p + 8 * k + 1) * pad, :]
            high = mat.astype(jnp.bfloat16).astype(jnp.float32)
            both.append(jnp.concatenate([high, mat - high], axis=0))
        lhs[p, :, 0:LANES] = jnp.where(wide < 2 * pad, both[0], both[1]).astype(jnp.bfloat16)
        lhs[p, :, LANES : 2 * LANES] = jnp.where(wide < 2 * pad, both[1], 0.0).astype(jnp.bfloat16)


def react_kernel(nspec, pad, counts, coef, cells, top, bottom, left, right, lhs, rate, out, state):
    rows_total = cells.shape[1]
    base = pl.program_id(0) * GROUP
    lane = lax.broadcasted_iota(jnp.int32, (GROUP, LANES), 1)
    sub = lax.broadcasted_iota(jnp.int32, (GROUP, LANES), 0)
    at_top = base == 0
    at_bottom = base + GROUP == rows_total
    row_above = jnp.maximum(base - 1, 0)
    row_below = jnp.minimum(base + GROUP, rows_total - 1)
    edge_cols = jnp.where(
        lane % 2 == 0,
        pltpu.roll(left[pl.ds(base, GROUP), :], 1, 1),
        pltpu.roll(right[pl.ds(base, GROUP), :], LANES - 1, 1),
    )

    for s in range(nspec, pad):
        state[pl.ds(s, GROUP, stride=pad), :] = jnp.zeros((GROUP, LANES), jnp.float32)
    for s in range(nspec):
        here = cells[s, pl.ds(base, GROUP), :]
        before = jnp.where(at_top, top[s : s + 1, :], cells[s, pl.ds(row_above, 1), :])
        after = jnp.where(at_bottom, bottom[s : s + 1, :], cells[s, pl.ds(row_below, 1), :])
        above = jnp.where(sub == 0, before, pltpu.roll(here, 1, 0))
        below = jnp.where(sub == GROUP - 1, after, pltpu.roll(here, GROUP - 1, 0))
        edge = pltpu.roll(edge_cols, LANES - 2 * s, 1) if s else edge_cols
        from_l = jnp.where(lane == 0, edge, pltpu.roll(here, 1, 1))
        from_r = jnp.where(lane == LANES - 1, edge, pltpu.roll(here, LANES - 1, 1))
        moved = here + coef[s] * ((above + below) + (from_l + from_r) - 4.0 * here)
        state[pl.ds(s, GROUP, stride=pad), :] = moved

    most = counts[base]
    for g in range(1, GROUP):
        most = jnp.maximum(most, counts[base + g])

    odd_rows = jnp.zeros((8, LANES), jnp.float32)
    nothing = jnp.zeros((2 * pad, LANES), jnp.bfloat16)
    unused = jnp.zeros((2 * LANES - 4 * pad, 2 * LANES), jnp.bfloat16)

    def parts(g):
        now = state[g * pad : (g + 1) * pad, :]
        pushed = now + rate[g : g + 1, :] * jnp.tanh(now)
        high = jnp.concatenate([pushed, odd_rows], axis=0).astype(jnp.bfloat16).astype(jnp.float32)[0:pad]
        return jnp.concatenate([high, pushed - high], axis=0).astype(jnp.bfloat16)

    def substep(step):
        for p in range(GROUP // 2):
            ends = (p // 8 * 16 + p % 8, p // 8 * 16 + p % 8 + 8)
            rhs = jnp.concatenate(
                [
                    jnp.concatenate([parts(ends[0]), nothing], axis=1),
                    jnp.concatenate([nothing, parts(ends[1])], axis=1),
                    unused,
                ],
                axis=0,
            )
            sums = jnp.dot(lhs[p], rhs, preferred_element_type=jnp.float32)
            sums = sums[0:pad] + sums[pad : 2 * pad]
            for k, g in enumerate(ends):
                mask = jnp.broadcast_to(step < counts[base + g], (pad, LANES))
                pltpu.store(state.at[pl.ds(g * pad, pad), :], sums[:, k * LANES : (k + 1) * LANES], mask=mask)

    def run(count, trips, start):
        def steps(i, step):
            for u in range(count):
                substep(step + u)
            return step + count

        return lax.fori_loop(0, trips, steps, start)

    most = jnp.where(most == 27, 28, most)
    done = run(15, jnp.maximum(most - 28, 0), 0)
    for count in UNROLLS:
        done = run(count, (most - done) // count, done)

    for s in range(nspec):
        out[s] = state[pl.ds(s, GROUP, stride=pad), :]


def body(species, diffusivity, propagator, reaction_rate, substeps):
    rows, nspec, lanes = species.shape
    pad = (nspec + 7) // 8 * 8
    f32 = jnp.float32
    cells = species.transpose(1, 0, 2)

    def shift(values, axis, up):
        count = lax.axis_size(axis)
        pairs = [(i, (i + 1) % count) if up else ((i + 1) % count, i) for i in range(count)]
        return lax.ppermute(values, axis, pairs)

    whole = pl.BlockSpec(memory_space=pltpu.VMEM)
    near, cols, first_row, last_row = pl.pallas_call(
        functools.partial(edges_kernel, nspec),
        name="edges",
        in_specs=[pl.BlockSpec(memory_space=pltpu.HBM)],
        out_specs=[whole] * 4,
        out_shape=[jax.ShapeDtypeStruct((nspec, rows, lanes), f32), jax.ShapeDtypeStruct((rows, lanes), f32)]
        + [jax.ShapeDtypeStruct((nspec, lanes), f32)] * 2,
        scratch_shapes=[pltpu.SemaphoreType.DMA((CHUNKS,))],
        compiler_params=pltpu.CompilerParams(vmem_limit_bytes=8 << 20),
        cost_estimate=pl.CostEstimate(flops=1 << 20, bytes_accessed=4 << 20, transcendentals=0),
    )(pltpu.with_memory_space_constraint(cells, pltpu.HBM))

    left = shift(cols, "pencil", True)
    right = shift(cols, "pencil", False)
    top = shift(last_row, "space", True)
    bottom = shift(first_row, "space", False)

    lhs = pl.pallas_call(
        functools.partial(matrices_kernel, nspec, pad),
        name="matrices",
        grid=(rows // PREP_ROWS,),
        in_specs=[pl.BlockSpec((PREP_ROWS, nspec * nspec), lambda i: (i, 0))],
        out_specs=pl.BlockSpec((PREP_ROWS // 2, 2 * pad, 2 * lanes), lambda i: (i, 0, 0)),
        out_shape=jax.ShapeDtypeStruct((rows // 2, 2 * pad, 2 * lanes), jnp.bfloat16),
        scratch_shapes=[pltpu.VMEM((PREP_ROWS * pad, lanes), f32)],
        compiler_params=pltpu.CompilerParams(vmem_limit_bytes=8 << 20),
        cost_estimate=pl.CostEstimate(flops=1 << 24, bytes_accessed=6 << 20, transcendentals=0),
    )(propagator)

    once = pl.Buffered(1)
    result = pl.pallas_call(
        functools.partial(react_kernel, nspec, pad),
        name="react",
        out_shape=jax.ShapeDtypeStruct((nspec, rows, lanes), f32),
        grid_spec=pltpu.PrefetchScalarGridSpec(
            num_scalar_prefetch=2,
            grid=(rows // GROUP,),
            in_specs=[
                pl.BlockSpec((nspec, rows, lanes), lambda i, c, d: (0, 0, 0), pipeline_mode=once),
                pl.BlockSpec((nspec, lanes), lambda i, c, d: (0, 0), pipeline_mode=once),
                pl.BlockSpec((nspec, lanes), lambda i, c, d: (0, 0), pipeline_mode=once),
                pl.BlockSpec((rows, lanes), lambda i, c, d: (0, 0), pipeline_mode=once),
                pl.BlockSpec((rows, lanes), lambda i, c, d: (0, 0), pipeline_mode=once),
                pl.BlockSpec((GROUP // 2, 2 * pad, 2 * lanes), lambda i, c, d: (i, 0, 0)),
                pl.BlockSpec((GROUP, lanes), lambda i, c, d: (i, 0)),
            ],
            out_specs=pl.BlockSpec((nspec, GROUP, lanes), lambda i, c, d: (0, i, 0)),
            scratch_shapes=[pltpu.VMEM((GROUP * pad, lanes), f32)],
        ),
        compiler_params=pltpu.CompilerParams(vmem_limit_bytes=24 << 20),
        cost_estimate=pl.CostEstimate(flops=20 * rows * 2 * pad * 256 * 256, bytes_accessed=9 << 20, transcendentals=0),
    )(substeps.reshape(rows), diffusivity, near, top, bottom, left, right, lhs, reaction_rate)
    return result.transpose(1, 0, 2)


def solution(mesh):
    return jax.shard_map(
        body,
        mesh=mesh,
        in_specs=(
            P("space", None, "pencil"),
            P(),
            P("space", "pencil"),
            P("space", "pencil"),
            P("space", "pencil"),
        ),
        out_specs=P("space", None, "pencil"),
        check_vma=False,
    )
```
